128 devices in a mesh: bf: 8 (over y_lo, z), sk: 16 (over x, y_hi, core).
Axes of the slice: x: 4, y: 4 (y_hi: 2, y_lo: 2; y = y_hi * 2 + y_lo), z: 4, core: 2. Of those that a mesh axis runs over, the one named last changes fastest.
Arguments:
- kernel: bfloat16 [2, 16384, 32768], P(None, 'bf', 'sk'), may hold values from -1.1048543 to 1.1048543
- sketch: bfloat16 [3, 32768, 256], P(None, 'sk'), may hold values from -6 to 6
- projections: bfloat16 [2, 8, 2, 256, 128], P(None, 'bf'), may hold values from -0.375 to 0.375
- inverses: bfloat16 [2, 8, 2, 256, 256], P(None, 'bf'), may hold values from -0.375 to 0.375
- norm_gain: float32 [256], replicated, may hold values from 0.5 to 1.5
Outputs:
- factor_sketch: float32 [2, 3, 16384, 256], P(None, None, ('bf', 'sk'))
The draws below stay inside these ranges and needn't reach their ends.
All inputs are finite; a program needn't handle non-finite values.
Results may differ from the reference program's by a relative error of at most 0.02.
Values may be sent and summed in bfloat16 or wider, within the bound.
A program may use at most 128 MiB of HBM per device.

```python
import math
import jax
import jax.numpy as jnp
from jax import lax

ROWS = 2048
SKETCH = 256
RANK = 128
PASSES = 3
LEVELS = 2
BLOCKS = 8
ROWS_ALL = 16384
COLS_ALL = 32768
N_BF = 8


def draw_kernel(key, part):
    key_rows = jax.random.fold_in(key, 11)
    key_cols = jax.random.fold_in(key, 12)
    key_vals = jax.random.fold_in(key, 13)
    col_scale = jnp.exp(jax.random.uniform(key_cols, (1, 1, COLS_ALL), jnp.float32, 0.0, math.log(10.0)))
    row_scale = jnp.exp(jax.random.uniform(key_rows, (1, ROWS_ALL, 1), jnp.float32, 0.0, math.log(10.0)))
    entries = jax.random.truncated_normal(key_vals, -6.0, 6.0, (2, ROWS_ALL, COLS_ALL), jnp.float32)
    values = entries * row_scale * col_scale / (3.0 * math.sqrt(COLS_ALL))
    return values.astype(jnp.bfloat16)


def level_of(stream_key, extent, cuts, low, largest):
    def one(position, blocks):
        draws = jax.random.uniform(jax.random.fold_in(jax.random.fold_in(stream_key, 6), position), (blocks,), jnp.float32, low / len(cuts), largest / len(cuts))
        return jnp.repeat(jnp.exp(draws), extent[position] // blocks).reshape((-1,) + (1,) * (len(extent) - position - 1))

    gain = one(*cuts[0])
    for cut in cuts[1:]:
        gain = gain * one(*cut)
    return gain


def gaussian(stream_key, shape, deviation, most, shards=(), kind=jnp.bfloat16):
    drawn = jax.random.normal(stream_key, shape, jnp.float32) * deviation
    if len(shards) > 0:
        drawn = level_of(stream_key, shape, shards, -0.22, 0.18) * drawn
    return jnp.clip(drawn, min=-most, max=most).astype(kind)


def setup_inputs(seed: int = 0) -> dict:
    keys = jax.random.split(jax.random.key(seed), 6)
    return {
        "kernel": draw_kernel(jax.random.fold_in(keys[5], 71), 0),
        "sketch": gaussian(keys[1], (PASSES, COLS_ALL, SKETCH), 1.0, 6.0, ((1, 16),)),
        "projections": gaussian(keys[2], (LEVELS, BLOCKS, 2, SKETCH, RANK), SKETCH ** -0.5, 0.375, ((1, 8),)),
        "inverses": gaussian(keys[3], (LEVELS, BLOCKS, 2, 2 * RANK, SKETCH), (2 * RANK) ** -0.5, 0.375, ((1, 8),)),
        "norm_gain": jnp.clip(1.0 + 0.1 * jax.random.normal(keys[4], (SKETCH,), jnp.float32), 0.5, 1.5),
    }


epsilon = 1e-06

def complex_level(real_in, imag_in, real_mat, imag_mat):
    real_in = real_in.astype(jnp.float32)
    imag_in = imag_in.astype(jnp.float32)
    real_mat = real_mat.astype(jnp.float32)
    imag_mat = imag_mat.astype(jnp.float32)
    real_out = jnp.einsum('pbrs,bsk->pbrk', real_in, real_mat) - jnp.einsum('pbrs,bsk->pbrk', imag_in, imag_mat)
    imag_out = jnp.einsum('pbrs,bsk->pbrk', real_in, imag_mat) + jnp.einsum('pbrs,bsk->pbrk', imag_in, real_mat)
    return (real_out, imag_out)

def reference(kernel, sketch, projections, inverses, norm_gain):
    real_blocks = []
    imag_blocks = []
    for block_idx in range(N_BF):
        kernel_re = kernel[0, block_idx * ROWS:(block_idx + 1) * ROWS]
        kernel_im = kernel[1, block_idx * ROWS:(block_idx + 1) * ROWS]
        proj_re = projections[0, block_idx, 0]
        proj_im = projections[0, block_idx, 1]
        real_pass = []
        imag_pass = []
        for pass_idx in range(PASSES):
            sk_re = jnp.dot(sketch[pass_idx], proj_re, preferred_element_type=jnp.float32).astype(jnp.bfloat16)
            sk_im = jnp.dot(sketch[pass_idx], proj_im, preferred_element_type=jnp.float32).astype(jnp.bfloat16)
            part_re = jnp.dot(kernel_re, sk_re, preferred_element_type=jnp.float32) - jnp.dot(kernel_im, sk_im, preferred_element_type=jnp.float32)
            part_im = jnp.dot(kernel_re, sk_im, preferred_element_type=jnp.float32) + jnp.dot(kernel_im, sk_re, preferred_element_type=jnp.float32)
            real_pass.append(part_re)
            imag_pass.append(part_im)
        real_blocks.append(jnp.stack(real_pass))
        imag_blocks.append(jnp.stack(imag_pass))
    own_re = jnp.stack(real_blocks, axis=1).astype(jnp.bfloat16)
    own_im = jnp.stack(imag_blocks, axis=1).astype(jnp.bfloat16)
    top_bits = N_BF.bit_length() - 1
    current_re = None
    current_im = None
    for level_idx in range(LEVELS):
        level_bit = top_bits - 1 - level_idx
        if level_idx > 0:
            rounded_re = current_re.astype(jnp.bfloat16)
            rounded_im = current_im.astype(jnp.bfloat16)
            own_re, own_im = complex_level(rounded_re, rounded_im, projections[level_idx, :, 0], projections[level_idx, :, 1])
            own_re = own_re.astype(jnp.bfloat16)
            own_im = own_im.astype(jnp.bfloat16)
        stride = 2 ** level_bit
        partner_re = jnp.flip(own_re.reshape(PASSES, N_BF // (2 * stride), 2, stride, ROWS, RANK), axis=2).reshape(PASSES, N_BF, ROWS, RANK)
        partner_im = jnp.flip(own_im.reshape(PASSES, N_BF // (2 * stride), 2, stride, ROWS, RANK), axis=2).reshape(PASSES, N_BF, ROWS, RANK)
        stacked_re = jnp.concatenate([own_re, partner_re], axis=-1)
        stacked_im = jnp.concatenate([own_im, partner_im], axis=-1)
        current_re, current_im = complex_level(stacked_re, stacked_im, inverses[level_idx, :, 0], inverses[level_idx, :, 1])
    power = lax.optimization_barrier(jnp.mean(current_re * current_re + current_im * current_im, axis=-1, keepdims=True))
    inv_rms = 1.0 / jnp.sqrt(power + epsilon)
    out_re = (current_re * inv_rms * norm_gain).reshape(PASSES, N_BF * ROWS, SKETCH)
    out_im = (current_im * inv_rms * norm_gain).reshape(PASSES, N_BF * ROWS, SKETCH)
    return jnp.stack([out_re, out_im])
```

```python
import functools

import jax
import jax.numpy as jnp
from jax import lax
from jax.experimental import pallas as pl
from jax.experimental.pallas import tpu as pltpu
from jax.sharding import Mesh
from jax.sharding import PartitionSpec as P

AXES = ("yl", "z", "x", "yh", "c")
MESH = pl.DeviceIdType.MESH
F32 = jnp.float32
BF16 = jnp.bfloat16
EPSILON = 1e-06


def complex_block(real, imag):
    upper = jnp.concatenate([real, imag], axis=1)
    lower = jnp.concatenate([-imag, real], axis=1)
    return jnp.concatenate([upper, lower], axis=0)


def dot(a, b):
    return jnp.dot(a, b, preferred_element_type=F32)


def kernel(
    k_hbm, s_hbm, proj_hbm, inv_hbm, gain_hbm, o_hbm,
    kv, sv, sp, projv, invv, gainv, mats, mats_far, last_mats,
    own, c_send, c_recv, x_send, x_recv,
    half, y1_send, y1_recv, held, y2_send, y2_recv, own1, z_recv, outv,
    k_sem, s_sem, w_sem, o_sem, m_sems, c_sems, x_sems, y1_sems, y2_sems, z_sems,
):
    yl, z, x, yh, c = (lax.axis_index(a) for a in AXES)
    passes = 3
    far_x = lax.rem(x + 2, 4)
    right = lax.rem(x + 1, 4)
    left = lax.rem(x + 3, 4)
    core_peer = (yl, z, x, yh, 1 - c)
    right_peer = (yl, z, right, yh, c)
    left_peer = (yl, z, left, yh, c)
    y1_peer = (1 - yl, z, x, 1 - yh, c)
    y2_peer = (1 - yl, z, x, yh, c)
    z_peer = (yl, lax.rem(z + 2, 4), x, yh, c)

    units = (
        ((far_x, 0), (far_x, 1)),
        ((right, 1), (left, 0)),
        ((right, 0), (left, 1)),
        ((x, 0), (x, 1)),
    )

    def k_copies(j):
        copies = []
        for part in range(2):
            for core, core_idx in enumerate((1 - c, c)):
                for u in range(2):
                    dest_x, dest_yh = units[j][u]
                    row = pl.multiple_of(((dest_x * 2 + dest_yh) * 2 + core_idx) * 128, 128)
                    copies.append(
                        pltpu.make_async_copy(
                            k_hbm.at[part, pl.ds(row, 128), :],
                            kv.at[j, part, pl.ds((core * 2 + u) * 128, 128), :],
                            k_sem.at[j, part, core * 2 + u],
                        )
                    )
        return copies

    def s_copy(p):
        return pltpu.make_async_copy(s_hbm.at[p], sv.at[p], s_sem.at[p])

    w_copies = (
        pltpu.make_async_copy(proj_hbm, projv, w_sem.at[0]),
        pltpu.make_async_copy(inv_hbm, invv, w_sem.at[1]),
        pltpu.make_async_copy(gain_hbm, gainv, w_sem.at[2]),
    )

    def remote(src, dst, sems, index, peer):
        return pltpu.make_async_remote_copy(
            src_ref=src,
            dst_ref=dst,
            send_sem=sems.at[(0,) + index],
            recv_sem=sems.at[(1,) + index],
            device_id=peer,
            device_id_type=MESH,
        )

    def m_copy():
        return remote(mats, mats_far, m_sems, (), y2_peer)

    def c_copy(p, j):
        return remote(c_send.at[p, j], c_recv.at[p, j], c_sems, (p, j), core_peer)

    def x_copy(p, j, u):
        peer = (right_peer, left_peer)[u]
        return remote(x_send.at[p, j, u], x_recv.at[p, j, u], x_sems, (p, j, u), peer)

    def y1_copy(p):
        return remote(y1_send.at[p], y1_recv.at[p], y1_sems, (p,), y1_peer)

    def y2_copy(p):
        return remote(y2_send.at[p], y2_recv.at[p], y2_sems, (p,), y2_peer)

    def z_copy(p):
        return remote(own1.at[p], z_recv.at[p], z_sems, (p,), z_peer)

    def o_copy(p):
        return pltpu.make_async_copy(outv.at[p], o_hbm.at[:, p], o_sem.at[p])

    w_copies[0].start()
    s_copy(0).start()
    for copy in k_copies(0):
        copy.start()
    w_copies[1].start()
    w_copies[2].start()
    for copy in k_copies(1):
        copy.start()
    s_copy(1).start()
    for copy in k_copies(2):
        copy.start()
    for copy in k_copies(3):
        copy.start()
    s_copy(2).start()

    barrier = pltpu.get_barrier_semaphore()
    for peer in (core_peer, right_peer, left_peer, y1_peer, y2_peer, z_peer):
        pl.semaphore_signal(barrier, inc=1, device_id=peer, device_id_type=MESH)

    def project(p):
        s_copy(p).wait()
        both = jnp.concatenate([projv[0, 0, 0], projv[0, 0, 1]], axis=1)
        for step in range(4):
            rows = pl.ds(step * 512, 512)
            part = dot(sv[p, rows, :], both).astype(BF16)
            sp[p, 0, rows, :] = part
            sp[p, 1, rows, :] = jnp.concatenate([-part[:, 128:], part[:, :128]], axis=1)

    w_copies[0].wait()
    project(0)
    w_copies[1].wait()
    w_copies[2].wait()
    level = complex_block(projv[1, 0, 0], projv[1, 0, 1])
    for i in range(2):
        rows = pl.ds(i * 128, 128)
        first = complex_block(invv[0, 0, 0, rows, :], invv[0, 0, 1, rows, :])
        mats[i] = dot(first, level).astype(BF16)
        last_mats[i] = complex_block(invv[1, 0, 0, rows, :], invv[1, 0, 1, rows, :])
    pl.semaphore_wait(barrier, 6)
    m_copy().start()

    def post(p, j):
        copy = c_copy(p, j)
        copy.wait_send()
        copy.wait_recv()
        for u in range(2):
            rows = pl.ds(u * 128, 128)
            unit = own[j, rows, :] + c_recv[p, j, rows, :].astype(F32)
            if j == 2:
                x_copy(p, 0, u).wait_recv()
                unit = unit + x_recv[p, 0, u].astype(F32)
            x_send[p, j, u] = unit.astype(BF16)
            x_copy(p, j, u).start()

    def finish_x(p):
        copy = c_copy(p, 3)
        copy.wait_send()
        copy.wait_recv()
        for j in (1, 2):
            for u in range(2):
                x_copy(p, j, u).wait_recv()
        for u in range(2):
            rows = pl.ds(u * 128, 128)
            half[u] = (
                own[3, rows, :]
                + c_recv[p, 3, rows, :].astype(F32)
                + x_recv[p, 2 - u, 0].astype(F32)
                + x_recv[p, 1 + u, 1].astype(F32)
            ).astype(BF16)
        y1_send[p] = half[1 - yh]
        y1_copy(p).start()
        held[p, 0] = half[yh].astype(F32)

    def level_products(p):
        y1_copy(p).wait_recv()
        mine = held[p, 0].astype(BF16)
        other = y1_recv[p]
        y2_send[p] = (dot(mine, mats_far[1]) + dot(other, mats_far[0])).astype(BF16)
        y2_copy(p).start()
        held[p, 1] = dot(mine, mats[0]) + dot(other, mats[1])

    def level_own(p):
        y2_copy(p).wait_recv()
        own1[p] = (held[p, 1] + y2_recv[p].astype(F32)).astype(BF16)
        z_copy(p).start()

    def finish(p):
        z_copy(p).wait_recv()
        current = dot(own1[p], last_mats[0]) + dot(z_recv[p], last_mats[1])
        power = jnp.sum(current * current, axis=-1, keepdims=True) / 256
        scaled = current * lax.rsqrt(power + EPSILON)
        gain = gainv[...]
        outv[p, 0] = scaled[:, :256] * gain
        outv[p, 1] = scaled[:, 256:] * gain
        o_copy(p).start()

    def slab(g, _):
        p = g // 4
        j = lax.rem(g, 4)

        for first in range(4):

            @pl.when(g == first)
            def _():
                for copy in k_copies(first):
                    copy.wait()

        acc = dot(kv[j, 0], sp[p, 0]) + dot(kv[j, 1], sp[p, 1])
        c_send[p, j] = acc[:256].astype(BF16)
        c_copy(p, j).start()
        own[j] = acc[256:]

        for ahead in (1, 2):

            @pl.when(g == 4 * ahead - 4)
            def _():
                project(ahead)

        @pl.when(j == 1)
        def _():
            post(p, 0)

        @pl.when(j == 2)
        def _():
            post(p, 1)

        @pl.when(j == 3)
        def _():
            post(p, 2)

        @pl.when((j == 1) & (p >= 1))
        def _():
            finish_x(p - 1)

        @pl.when((j == 1) & (p >= 2))
        def _():
            level_own(p - 2)

        @pl.when((j == 3) & (p == 1))
        def _():
            m_copy().wait_recv()

        @pl.when((j == 3) & (p >= 1))
        def _():
            level_products(p - 1)

        return 0

    lax.fori_loop(0, 4 * passes, slab, 0)
    finish(0)
    finish_x(2)
    level_own(1)
    level_products(2)
    finish(1)
    level_own(2)
    finish(2)
    m_copy().wait_send()
    for p in range(passes):
        for u in range(2):
            for j in range(3):
                x_copy(p, j, u).wait_send()
        y1_copy(p).wait_send()
        y2_copy(p).wait_send()
        z_copy(p).wait_send()
        o_copy(p).wait()


def shards(kernel_shard, sketch, projections, inverses, norm_gain):
    dma = pltpu.SemaphoreType.DMA
    return pl.pallas_call(
        kernel,
        out_shape=jax.ShapeDtypeStruct((2, 3, 128, 256), F32),
        in_specs=[pl.BlockSpec(memory_space=pl.ANY)] * 5,
        out_specs=pl.BlockSpec(memory_space=pl.ANY),
        scratch_shapes=[
            pltpu.VMEM((4, 2, 512, 2048), BF16),
            pltpu.VMEM((3, 2048, 256), BF16),
            pltpu.VMEM((3, 2, 2048, 256), BF16),
            pltpu.VMEM((2, 1, 2, 256, 128), BF16),
            pltpu.VMEM((2, 1, 2, 256, 256), BF16),
            pltpu.VMEM((1, 256), F32),
            pltpu.VMEM((2, 256, 256), BF16),
            pltpu.VMEM((2, 256, 256), BF16),
            pltpu.VMEM((2, 256, 512), BF16),
            pltpu.VMEM((4, 256, 256), F32),
            pltpu.VMEM((3, 4, 256, 256), BF16),
            pltpu.VMEM((3, 4, 256, 256), BF16),
            pltpu.VMEM((3, 3, 2, 128, 256), BF16),
            pltpu.VMEM((3, 3, 2, 128, 256), BF16),
            pltpu.VMEM((2, 128, 256), BF16),
            pltpu.VMEM((3, 128, 256), BF16),
            pltpu.VMEM((3, 128, 256), BF16),
            pltpu.VMEM((3, 2, 128, 256), F32),
            pltpu.VMEM((3, 128, 256), BF16),
            pltpu.VMEM((3, 128, 256), BF16),
            pltpu.VMEM((3, 128, 256), BF16),
            pltpu.VMEM((3, 128, 256), BF16),
            pltpu.VMEM((3, 2, 128, 256), F32),
            dma((4, 2, 4)),
            dma((3,)),
            dma((3,)),
            dma((3,)),
            dma((2,)),
            dma((2, 3, 4)),
            dma((2, 3, 3, 2)),
            dma((2, 3)),
            dma((2, 3)),
            dma((2, 3)),
        ],
        compiler_params=pltpu.CompilerParams(
            collective_id=0, has_side_effects=True, vmem_limit_bytes=56 << 20
        ),
        name="butterfly",
    )(kernel_shard, sketch, projections, inverses, norm_gain.reshape(1, 256))


def solution(mesh):
    torus = Mesh(mesh.devices.reshape(2, 4, 4, 2, 2), AXES)
    in_specs = (
        P(None, ("yl", "z"), ("x", "yh", "c")),
        P(None, ("x", "yh", "c"), None),
        P(None, ("yl", "z"), None, None, None),
        P(None, ("yl", "z"), None, None, None),
        P(),
    )
    return jax.shard_map(
        shards, mesh=torus, in_specs=in_specs, out_specs=P(None, None, AXES, None), check_vma=False
    )
```

```python
import jax
import jax.numpy as jnp
from jax import lax
from jax.experimental import pallas as pl
from jax.experimental.pallas import tpu as pltpu
from jax.sharding import Mesh
from jax.sharding import PartitionSpec as P

AXES = ("yl", "z", "x", "yh", "c")
MESH = pl.DeviceIdType.MESH
F32 = jnp.float32
BF16 = jnp.bfloat16
EPSILON = 1e-06
PASSES = 3
LAST = PASSES - 1


def complex_block(real, imag):
    upper = jnp.concatenate([real, imag], axis=1)
    lower = jnp.concatenate([-imag, real], axis=1)
    return jnp.concatenate([upper, lower], axis=0)


def dot(a, b):
    return jnp.dot(a, b, preferred_element_type=F32)


def span(p, h):
    return pl.ds(h * 64, 64) if p == LAST else pl.ds(0, 128)


def reduce_kernel(
    k_hbm, s_hbm, proj_hbm, inv_hbm, own1_out, far1_out, mats_out,
    kv, sv, pair, single, projv, invv, mats, mats_far,
    own, c_send, c_recv, x_send, x_recv,
    mine, y1_send, y1_recv, held, y2_send, y2_recv, own1, z_recv,
    k_sem, s_sem, w_sem, m_sems, c_sems, x_sems, y1_sems, y2_sems, z_sems,
):
    yl, z, x, yh, c = (lax.axis_index(a) for a in AXES)
    far_x = lax.rem(x + 2, 4)
    right = lax.rem(x + 1, 4)
    left = lax.rem(x + 3, 4)
    core_peer = (yl, z, x, yh, 1 - c)
    right_peer = (yl, z, right, yh, c)
    left_peer = (yl, z, left, yh, c)
    y1_peer = (1 - yl, z, x, 1 - yh, c)
    y2_peer = (1 - yl, z, x, yh, c)
    z_peer = (yl, lax.rem(z + 2, 4), x, yh, c)

    units = (
        ((far_x, 0), (far_x, 1)),
        ((right, 1), (left, 0)),
        ((right, 0), (left, 1)),
        ((x, 0), (x, 1)),
    )

    def start_slab(j):
        def start_part(part, _):
            for core, core_idx in enumerate((1 - c, c)):
                for u in range(2):
                    dest_x, dest_yh = units[j][u]
                    row = pl.multiple_of(((dest_x * 2 + dest_yh) * 2 + core_idx) * 128, 128)
                    pltpu.make_async_copy(
                        k_hbm.at[part, pl.ds(row, 128), :],
                        kv.at[j, part, pl.ds((core * 2 + u) * 128, 128), :],
                        k_sem.at[j],
                    ).start()
            return 0

        lax.fori_loop(0, 2, start_part, 0)

    def wait_slab(j):
        pltpu.make_async_copy(k_hbm.at[:, pl.ds(0, 512), :], kv.at[j], k_sem.at[j]).wait()

    def s_copy(p):
        return pltpu.make_async_copy(s_hbm.at[p], sv.at[p], s_sem.at[p])

    proj_copy = pltpu.make_async_copy(proj_hbm, projv, w_sem.at[0])
    inv_copy = pltpu.make_async_copy(inv_hbm, invv, w_sem.at[1])

    def remote(src, dst, sems, index, peer):
        return pltpu.make_async_remote_copy(
            src_ref=src,
            dst_ref=dst,
            send_sem=sems.at[(0,) + index],
            recv_sem=sems.at[(1,) + index],
            device_id=peer,
            device_id_type=MESH,
        )

    def m_copy():
        return remote(mats, mats_far, m_sems, (), y2_peer)

    def c_copy(p, j):
        return remote(c_send.at[p, j], c_recv.at[p, j], c_sems, (p, j), core_peer)

    def x_copy(p, j, u, h=0):
        peer = (right_peer, left_peer)[u]
        rows = span(p, h) if j == 2 else pl.ds(0, 128)
        at = (p, j, u, rows)
        return remote(x_send.at[at], x_recv.at[at], x_sems, (p, j + h, u), peer)

    def y1_copy(p, h):
        at = (p, span(p, h))
        return remote(y1_send.at[at], y1_recv.at[at], y1_sems, (p + h,), y1_peer)

    def y2_copy(p, h):
        at = (p, span(p, h))
        return remote(y2_send.at[at], y2_recv.at[at], y2_sems, (p + h,), y2_peer)

    def z_copy(p, h):
        at = (p, span(p, h))
        return remote(own1.at[at], z_recv.at[at], z_sems, (p + h,), z_peer)

    proj_copy.start()
    s_copy(0).start()
    s_copy(1).start()
    start_slab(0)
    inv_copy.start()
    start_slab(1)
    start_slab(2)
    start_slab(3)
    s_copy(2).start()

    barrier = pltpu.get_barrier_semaphore()
    for peer in (core_peer, right_peer, left_peer, y1_peer, y2_peer, z_peer):
        pl.semaphore_signal(barrier, inc=1, device_id=peer, device_id_type=MESH)

    proj_copy.wait()
    s_copy(0).wait()
    s_copy(1).wait()
    both = jnp.concatenate([projv[0, 0, 0], projv[0, 0, 1]], axis=1)
    for step in range(4):
        rows = pl.ds(step * 512, 512)
        first = dot(sv[0, rows, :], both).astype(BF16)
        second = dot(sv[1, rows, :], both).astype(BF16)
        real = jnp.concatenate([first[:, :128], second[:, :128]], axis=1)
        imag = jnp.concatenate([first[:, 128:], second[:, 128:]], axis=1)
        pair[0, rows, :] = real
        pair[1, rows, :] = imag
        pair[2, rows, :] = real + imag

    inv_copy.wait()
    level = complex_block(projv[1, 0, 0], projv[1, 0, 1])
    for i in range(2):
        rows = pl.ds(i * 128, 128)
        first = complex_block(invv[0, 0, 0, rows, :], invv[0, 0, 1, rows, :])
        mats[i] = dot(first, level).astype(BF16)
        mats_out[i] = complex_block(invv[1, 0, 0, rows, :], invv[1, 0, 1, rows, :])

    def project_last():
        s_copy(LAST).wait()
        both = jnp.concatenate([projv[0, 0, 0], projv[0, 0, 1]], axis=1)
        for step in range(4):
            rows = pl.ds(step * 512, 512)
            part = dot(sv[LAST, rows, :], both).astype(BF16)
            single[0, rows, :] = part
            single[1, rows, :] = jnp.concatenate([-part[:, 128:], part[:, :128]], axis=1)

    def post(p, j):
        copy = c_copy(p, j)
        copy.wait_send()
        copy.wait_recv()
        if j == 2:
            for u in range(2):
                x_copy(p, 0, u).wait_recv()
        for h in range(2 if p == LAST and j == 2 else 1):
            for u in range(2):
                rows = span(p, h) if j == 2 else pl.ds(0, 128)
                near = pl.ds(u * 128 + rows.start, rows.size)
                unit = own[p, j, near, :] + c_recv[p, j, near, :].astype(F32)
                if j == 2:
                    unit = unit + x_recv[p, 0, u, rows, :].astype(F32)
                x_send[p, j, u, rows, :] = unit.astype(BF16)
                x_copy(p, j, u, h).start()

    def finish_x(p, h):
        if h == 0:
            copy = c_copy(p, 3)
            copy.wait_send()
            copy.wait_recv()
            for u in range(2):
                x_copy(p, 1, u).wait_recv()
        for u in range(2):
            x_copy(p, 2, u, h).wait_recv()
        rows = span(p, h)

        def total(u):
            near = pl.ds(pl.multiple_of(u * 128 + rows.start, rows.size), rows.size)
            return (
                own[p, 3, near, :]
                + c_recv[p, 3, near, :].astype(F32)
                + x_recv[p, 2 - u, 0, rows, :].astype(F32)
                + x_recv[p, 1 + u, 1, rows, :].astype(F32)
            ).astype(BF16)

        y1_send[p, rows, :] = total(1 - yh)
        y1_copy(p, h).start()
        mine[p, rows, :] = total(yh)

    def level_products(p, h):
        y1_copy(p, h).wait_recv()
        rows = span(p, h)
        near = mine[p, rows, :]
        other = y1_recv[p, rows, :]
        y2_send[p, rows, :] = (dot(near, mats_far[1]) + dot(other, mats_far[0])).astype(BF16)
        y2_copy(p, h).start()
        held[p, rows, :] = dot(near, mats[0]) + dot(other, mats[1])

    def level_own(p, h):
        y2_copy(p, h).wait_recv()
        rows = span(p, h)
        value = (held[p, rows, :] + y2_recv[p, rows, :].astype(F32)).astype(BF16)
        own1[p, rows, :] = value
        z_copy(p, h).start()
        own1_out[p, rows, :] = value

    def finish(p, h):
        z_copy(p, h).wait_recv()
        rows = span(p, h)
        far1_out[p, rows, :] = z_recv[p, rows, :]

    def pair_slab(j, _):
        wait_slab(j)
        real_part = dot(kv[j, 0], pair[0])
        imag_part = dot(kv[j, 1], pair[1])
        cross = dot(kv[j, 0] + kv[j, 1], pair[2])
        real = real_part - imag_part
        imag = cross - real_part - imag_part

        @pl.when(j == 0)
        def _():
            pl.semaphore_wait(barrier, 6)

        for p in range(2):
            cols = slice(p * 128, (p + 1) * 128)
            acc = jnp.concatenate([real[:, cols], imag[:, cols]], axis=1)
            c_send[p, j] = acc[:256].astype(BF16)
            c_copy(p, j).start()
            own[p, j] = acc[256:]

        @pl.when(j == 0)
        def _():
            m_copy().start()

        for done in range(3):

            @pl.when(j == done + 1)
            def _():
                post(0, done)
                post(1, done)

        @pl.when(j == 2)
        def _():
            project_last()

        return 0

    def single_slab(j, _):
        acc = dot(kv[j, 0], single[0]) + dot(kv[j, 1], single[1])
        c_send[LAST, j] = acc[:256].astype(BF16)
        c_copy(LAST, j).start()
        own[LAST, j] = acc[256:]

        @pl.when(j == 1)
        def _():
            post(LAST, 0)

        @pl.when(j == 2)
        def _():
            post(LAST, 1)
            finish_x(0, 0)

        return 0

    lax.fori_loop(0, 4, pair_slab, 0)
    lax.fori_loop(0, 4, single_slab, 0)
    finish_x(1, 0)
    post(LAST, 2)
    m_copy().wait()
    level_products(0, 0)
    level_products(1, 0)
    finish_x(LAST, 0)
    finish_x(LAST, 1)
    level_own(0, 0)
    level_own(1, 0)
    level_products(LAST, 0)
    level_products(LAST, 1)
    level_own(LAST, 0)
    level_own(LAST, 1)
    finish(0, 0)
    finish(1, 0)
    finish(LAST, 0)
    finish(LAST, 1)
    for p in range(PASSES):
        for u in range(2):
            for j in range(3):
                x_copy(p, j, u).wait_send()
        y1_copy(p, 0).wait_send()
        y2_copy(p, 0).wait_send()
        z_copy(p, 0).wait_send()
    for u in range(2):
        x_copy(LAST, 2, u, 1).wait_send()
    y1_copy(LAST, 1).wait_send()
    y2_copy(LAST, 1).wait_send()
    z_copy(LAST, 1).wait_send()


def last_kernel(own1, far1, mats, gain, o_hbm, outv, o_sem):
    def o_copy(p):
        return pltpu.make_async_copy(outv.at[p], o_hbm.at[:, p], o_sem.at[p])

    for p in range(PASSES):
        current = dot(own1[p], mats[0]) + dot(far1[p], mats[1])
        power = jnp.sum(current * current, axis=-1, keepdims=True) / 256
        scaled = current * lax.rsqrt(power + EPSILON)
        outv[p, 0] = scaled[:, :256] * gain[...]
        outv[p, 1] = scaled[:, 256:] * gain[...]
        o_copy(p).start()
    for p in range(PASSES):
        o_copy(p).wait()


def shards(kernel_shard, sketch, projections, inverses, norm_gain):
    dma = pltpu.SemaphoreType.DMA
    vmem = pl.BlockSpec(memory_space=pltpu.VMEM)
    hbm = pl.BlockSpec(memory_space=pl.ANY)
    own1, far1, mats = pl.pallas_call(
        reduce_kernel,
        out_shape=(
            jax.ShapeDtypeStruct((3, 128, 256), BF16),
            jax.ShapeDtypeStruct((3, 128, 256), BF16),
            jax.ShapeDtypeStruct((2, 256, 512), BF16),
        ),
        in_specs=[hbm] * 4,
        out_specs=(vmem, vmem, vmem),
        scratch_shapes=[
            pltpu.VMEM((4, 2, 512, 2048), BF16),
            pltpu.VMEM((3, 2048, 256), BF16),
            pltpu.VMEM((3, 2048, 256), BF16),
            pltpu.VMEM((2, 2048, 256), BF16),
            pltpu.VMEM((2, 1, 2, 256, 128), BF16),
            pltpu.VMEM((2, 1, 2, 256, 256), BF16),
            pltpu.VMEM((2, 256, 256), BF16),
            pltpu.VMEM((2, 256, 256), BF16),
            pltpu.VMEM((3, 4, 256, 256), F32),
            pltpu.VMEM((3, 4, 256, 256), BF16),
            pltpu.VMEM((3, 4, 256, 256), BF16),
            pltpu.VMEM((3, 3, 2, 128, 256), BF16),
            pltpu.VMEM((3, 3, 2, 128, 256), BF16),
            pltpu.VMEM((3, 128, 256), BF16),
            pltpu.VMEM((3, 128, 256), BF16),
            pltpu.VMEM((3, 128, 256), BF16),
            pltpu.VMEM((3, 128, 256), F32),
            pltpu.VMEM((3, 128, 256), BF16),
            pltpu.VMEM((3, 128, 256), BF16),
            pltpu.VMEM((3, 128, 256), BF16),
            pltpu.VMEM((3, 128, 256), BF16),
            dma((4,)),
            dma((3,)),
            dma((2,)),
            dma((2,)),
            dma((2, 3, 4)),
            dma((2, 3, 4, 2)),
            dma((2, 4)),
            dma((2, 4)),
            dma((2, 4)),
        ],
        compiler_params=pltpu.CompilerParams(
            collective_id=0, has_side_effects=True, vmem_limit_bytes=56 << 20
        ),
        name="reduce_levels",
    )(kernel_shard, sketch, projections, inverses)
    return pl.pallas_call(
        last_kernel,
        out_shape=jax.ShapeDtypeStruct((2, 3, 128, 256), F32),
        in_specs=[vmem] * 4,
        out_specs=hbm,
        scratch_shapes=[pltpu.VMEM((3, 2, 128, 256), F32), dma((3,))],
        name="last_level",
    )(own1, far1, mats, norm_gain.reshape(1, 256))


def solution(mesh):
    torus = Mesh(mesh.devices.reshape(2, 4, 4, 2, 2), AXES)
    in_specs = (
        P(None, ("yl", "z"), ("x", "yh", "c")),
        P(None, ("x", "yh", "c"), None),
        P(None, ("yl", "z"), None, None, None),
        P(None, ("yl", "z"), None, None, None),
        P(),
    )
    return jax.shard_map(
        shards, mesh=torus, in_specs=in_specs, out_specs=P(None, None, AXES, None), check_vma=False
    )
```

```python
import jax
import jax.numpy as jnp
from jax import lax
from jax.experimental import pallas as pl
from jax.experimental.pallas import tpu as pltpu
from jax.sharding import Mesh
from jax.sharding import PartitionSpec as P

AXES = ("yl", "z", "x", "yh", "c")
MESH = pl.DeviceIdType.MESH
F32 = jnp.float32
BF16 = jnp.bfloat16
EPSILON = 1e-06
PASSES = 3
LAST = PASSES - 1


def complex_block(real, imag):
    upper = jnp.concatenate([real, imag], axis=1)
    lower = jnp.concatenate([-imag, real], axis=1)
    return jnp.concatenate([upper, lower], axis=0)


def dot(a, b):
    return jnp.dot(a, b, preferred_element_type=F32)


def span(p, h):
    return pl.ds(h * 64, 64) if p == LAST else pl.ds(0, 128)


def reduce_kernel(
    k_hbm, s_hbm, proj_hbm, inv_hbm, *refs,
):
    outs = refs[:6]
    (
        kv, sv, pair, single, projv, invv, mats, mats_far, last_mats,
        own, c_send, c_recv, x_send, x_recv,
        mine, y1_send, y1_recv, held, y2_send, y2_recv, own1, z_recv, near_last,
        k_sem, s_sem, w_sem, m_sems, c_sems, x_sems, y1_sems, y2_sems, z_sems,
) = refs[6:]
    yl, z, x, yh, c = (lax.axis_index(a) for a in AXES)
    far_x = lax.rem(x + 2, 4)
    right = lax.rem(x + 1, 4)
    left = lax.rem(x + 3, 4)
    core_peer = (yl, z, x, yh, 1 - c)
    right_peer = (yl, z, right, yh, c)
    left_peer = (yl, z, left, yh, c)
    y1_peer = (1 - yl, z, x, 1 - yh, c)
    y2_peer = (1 - yl, z, x, yh, c)
    z_peer = (yl, lax.rem(z + 2, 4), x, yh, c)

    units = (
        ((far_x, 0), (far_x, 1)),
        ((right, 1), (left, 0)),
        ((right, 0), (left, 1)),
        ((x, 0), (x, 1)),
    )

    def start_slab(j):
        def start_half(half, _):
            core = 1 - c + half * (2 * c - 1)
            for part in range(2):
                for u in range(2):
                    dest_x, dest_yh = units[j][u]
                    row = pl.multiple_of(((dest_x * 2 + dest_yh) * 2 + core) * 128, 128)
                    near = pl.multiple_of((half * 2 + u) * 128, 128)
                    pltpu.make_async_copy(
                        k_hbm.at[part, pl.ds(row, 128), :],
                        kv.at[j, part, pl.ds(near, 128), :],
                        k_sem.at[j, half],
                    ).start()
            return 0

        lax.fori_loop(0, 2, start_half, 0)

    def wait_slab(j, half):
        pltpu.make_async_copy(
            k_hbm.at[:, pl.ds(0, 256), :],
            kv.at[j, :, pl.ds(half * 256, 256), :],
            k_sem.at[j, half],
        ).wait()

    def s_copy(p):
        return pltpu.make_async_copy(s_hbm.at[p], sv.at[p], s_sem.at[p])

    proj_copy = pltpu.make_async_copy(proj_hbm, projv, w_sem.at[0])
    inv_copy = pltpu.make_async_copy(inv_hbm, invv, w_sem.at[1])

    def remote(src, dst, sems, index, peer):
        return pltpu.make_async_remote_copy(
            src_ref=src,
            dst_ref=dst,
            send_sem=sems.at[(0,) + index],
            recv_sem=sems.at[(1,) + index],
            device_id=peer,
            device_id_type=MESH,
        )

    def m_copy():
        return remote(mats, mats_far, m_sems, (), y2_peer)

    def c_copy(p, j):
        return remote(c_send.at[p, j], c_recv.at[p, j], c_sems, (p, j), core_peer)

    def x_copy(p, j, u, h=0):
        peer = (right_peer, left_peer)[u]
        rows = span(p, h) if j == 2 else pl.ds(0, 128)
        at = (p, j, u, rows)
        return remote(x_send.at[at], x_recv.at[at], x_sems, (p, j + h, u), peer)

    def y1_copy(p, h):
        at = (p, span(p, h))
        return remote(y1_send.at[at], y1_recv.at[at], y1_sems, (p + h,), y1_peer)

    def y2_copy(p, h):
        at = (p, span(p, h))
        return remote(y2_send.at[at], y2_recv.at[at], y2_sems, (p + h,), y2_peer)

    def z_copy(p, h):
        at = (p, span(p, h))
        return remote(own1.at[at], z_recv.at[at], z_sems, (p + h,), z_peer)

    proj_copy.start()
    s_copy(0).start()
    s_copy(1).start()
    start_slab(0)
    inv_copy.start()
    start_slab(1)
    start_slab(2)
    start_slab(3)
    s_copy(2).start()

    barrier = pltpu.get_barrier_semaphore()
    for peer in (core_peer, right_peer, left_peer, y1_peer, y2_peer, z_peer):
        pl.semaphore_signal(barrier, inc=1, device_id=peer, device_id_type=MESH)

    proj_copy.wait()
    s_copy(0).wait()
    s_copy(1).wait()
    both = jnp.concatenate([projv[0, 0, 0], projv[0, 0, 1]], axis=1)
    for step in range(4):
        rows = pl.ds(step * 512, 512)
        first = dot(sv[0, rows, :], both).astype(BF16)
        second = dot(sv[1, rows, :], both).astype(BF16)
        real = jnp.concatenate([first[:, :128], second[:, :128]], axis=1)
        imag = jnp.concatenate([first[:, 128:], second[:, 128:]], axis=1)
        pair[0, rows, :] = real
        pair[1, rows, :] = imag
        pair[2, rows, :] = real + imag

    inv_copy.wait()
    level = complex_block(projv[1, 0, 0], projv[1, 0, 1])
    for i in range(2):
        rows = pl.ds(i * 128, 128)
        first = complex_block(invv[0, 0, 0, rows, :], invv[0, 0, 1, rows, :])
        mats[i] = dot(first, level).astype(BF16)
        last_mats[i] = complex_block(invv[1, 0, 0, rows, :], invv[1, 0, 1, rows, :])

    def project_last():
        s_copy(LAST).wait()
        both = jnp.concatenate([projv[0, 0, 0], projv[0, 0, 1]], axis=1)
        for step in range(4):
            rows = pl.ds(step * 512, 512)
            part = dot(sv[LAST, rows, :], both).astype(BF16)
            single[0, rows, :] = part
            single[1, rows, :] = jnp.concatenate([-part[:, 128:], part[:, :128]], axis=1)

    def post(p, j):
        copy = c_copy(p, j)
        copy.wait_send()
        copy.wait_recv()
        if j == 2:
            for u in range(2):
                x_copy(p, 0, u).wait_recv()
        for h in range(2 if p == LAST and j == 2 else 1):
            for u in range(2):
                rows = span(p, h) if j == 2 else pl.ds(0, 128)
                near = pl.ds(u * 128 + rows.start, rows.size)
                unit = own[p, j, near, :] + c_recv[p, j, near, :].astype(F32)
                if j == 2:
                    unit = unit + x_recv[p, 0, u, rows, :].astype(F32)
                x_send[p, j, u, rows, :] = unit.astype(BF16)
                x_copy(p, j, u, h).start()

    def finish_x(p, h):
        if h == 0:
            copy = c_copy(p, 3)
            copy.wait_send()
            copy.wait_recv()
            for u in range(2):
                x_copy(p, 1, u).wait_recv()
        for u in range(2):
            x_copy(p, 2, u, h).wait_recv()
        rows = span(p, h)

        def total(u):
            near = pl.ds(pl.multiple_of(u * 128 + rows.start, rows.size), rows.size)
            return (
                own[p, 3, near, :]
                + c_recv[p, 3, near, :].astype(F32)
                + x_recv[p, 2 - u, 0, rows, :].astype(F32)
                + x_recv[p, 1 + u, 1, rows, :].astype(F32)
            ).astype(BF16)

        y1_send[p, rows, :] = total(1 - yh)
        y1_copy(p, h).start()
        mine[p, rows, :] = total(yh)

    def level_products(p, h):
        y1_copy(p, h).wait_recv()
        rows = span(p, h)
        near = mine[p, rows, :]
        other = y1_recv[p, rows, :]
        y2_send[p, rows, :] = (dot(near, mats_far[1]) + dot(other, mats_far[0])).astype(BF16)
        y2_copy(p, h).start()
        held[p, rows, :] = dot(near, mats[0]) + dot(other, mats[1])

    def level_own(p, h):
        y2_copy(p, h).wait_recv()
        rows = span(p, h)
        value = (held[p, rows, :] + y2_recv[p, rows, :].astype(F32)).astype(BF16)
        own1[p, rows, :] = value
        z_copy(p, h).start()
        near_last[p, rows, :] = dot(value, last_mats[0])

    def finish(p, h):
        z_copy(p, h).wait_recv()
        rows = span(p, h)
        value = near_last[p, rows, :] + dot(z_recv[p, rows, :], last_mats[1])
        outs[2 * p][rows, :] = value[:, :256]
        outs[2 * p + 1][rows, :] = value[:, 256:]

    def pair_slab(j, _):
        wait_slab(j, 0)
        wait_slab(j, 1)
        real_part = dot(kv[j, 0], pair[0])
        imag_part = dot(kv[j, 1], pair[1])
        cross = dot(kv[j, 0] + kv[j, 1], pair[2])
        real = real_part - imag_part
        imag = cross - real_part - imag_part
        for p in range(2):
            cols = slice(p * 128, (p + 1) * 128)
            acc = jnp.concatenate([real[:, cols], imag[:, cols]], axis=1)
            c_send[p, j] = acc[:256].astype(BF16)
            own[p, j] = acc[256:]

        @pl.when(j == 0)
        def _():
            pl.semaphore_wait(barrier, 6)

        for p in range(2):
            c_copy(p, j).start()

        @pl.when(j == 0)
        def _():
            m_copy().start()
            post(0, 0)
            post(1, 0)

        for done in (1, 2):

            @pl.when(j == done + 1)
            def _():
                post(0, done)
                post(1, done)

        @pl.when(j == 2)
        def _():
            project_last()

        return 0

    def single_slab(j, _):
        acc = dot(kv[j, 0], single[0]) + dot(kv[j, 1], single[1])
        c_send[LAST, j] = acc[:256].astype(BF16)
        c_copy(LAST, j).start()
        own[LAST, j] = acc[256:]

        for done in range(3):

            @pl.when(j == done + 1)
            def _():
                post(LAST, done)

        for p in range(2):

            @pl.when(j == p + 1)
            def _():
                finish_x(p, 0)

        return 0

    lax.fori_loop(0, 4, pair_slab, 0)
    lax.fori_loop(0, 4, single_slab, 0)
    m_copy().wait()
    level_products(0, 0)
    level_products(1, 0)
    finish_x(LAST, 0)
    finish_x(LAST, 1)
    level_own(0, 0)
    level_own(1, 0)
    level_products(LAST, 0)
    level_products(LAST, 1)
    finish(0, 0)
    level_own(LAST, 0)
    level_own(LAST, 1)
    finish(1, 0)
    finish(LAST, 0)
    finish(LAST, 1)
    for p in range(PASSES):
        for u in range(2):
            for j in range(3):
                x_copy(p, j, u).wait_send()
        y1_copy(p, 0).wait_send()
        y2_copy(p, 0).wait_send()
        z_copy(p, 0).wait_send()
    for u in range(2):
        x_copy(LAST, 2, u, 1).wait_send()
    y1_copy(LAST, 1).wait_send()
    y2_copy(LAST, 1).wait_send()
    z_copy(LAST, 1).wait_send()


def last_kernel(*refs):
    gain, o_hbm, outv, o_sem = refs[6:]

    def o_copy(p):
        return pltpu.make_async_copy(outv.at[p], o_hbm.at[:, p], o_sem.at[p])

    for p in range(PASSES):
        real, imag = refs[2 * p][...], refs[2 * p + 1][...]
        power = jnp.sum(real * real + imag * imag, axis=-1, keepdims=True) / 256
        scale = lax.rsqrt(power + EPSILON)
        outv[p, 0] = real * scale * gain[...]
        outv[p, 1] = imag * scale * gain[...]
        o_copy(p).start()
    for p in range(PASSES):
        o_copy(p).wait()


def shards(kernel_shard, sketch, projections, inverses, norm_gain):
    dma = pltpu.SemaphoreType.DMA
    vmem = pl.BlockSpec(memory_space=pltpu.VMEM)
    hbm = pl.BlockSpec(memory_space=pl.ANY)
    current = pl.pallas_call(
        reduce_kernel,
        out_shape=[jax.ShapeDtypeStruct((128, 256), F32)] * 6,
        in_specs=[hbm] * 4,
        out_specs=[vmem] * 6,
        scratch_shapes=[
            pltpu.VMEM((4, 2, 512, 2048), BF16),
            pltpu.VMEM((3, 2048, 256), BF16),
            pltpu.VMEM((3, 2048, 256), BF16),
            pltpu.VMEM((2, 2048, 256), BF16),
            pltpu.VMEM((2, 1, 2, 256, 128), BF16),
            pltpu.VMEM((2, 1, 2, 256, 256), BF16),
            pltpu.VMEM((2, 256, 256), BF16),
            pltpu.VMEM((2, 256, 256), BF16),
            pltpu.VMEM((2, 256, 512), BF16),
            pltpu.VMEM((3, 4, 256, 256), F32),
            pltpu.VMEM((3, 4, 256, 256), BF16),
            pltpu.VMEM((3, 4, 256, 256), BF16),
            pltpu.VMEM((3, 3, 2, 128, 256), BF16),
            pltpu.VMEM((3, 3, 2, 128, 256), BF16),
            pltpu.VMEM((3, 128, 256), BF16),
            pltpu.VMEM((3, 128, 256), BF16),
            pltpu.VMEM((3, 128, 256), BF16),
            pltpu.VMEM((3, 128, 256), F32),
            pltpu.VMEM((3, 128, 256), BF16),
            pltpu.VMEM((3, 128, 256), BF16),
            pltpu.VMEM((3, 128, 256), BF16),
            pltpu.VMEM((3, 128, 256), BF16),
            pltpu.VMEM((3, 128, 512), F32),
            dma((4, 2)),
            dma((3,)),
            dma((2,)),
            dma((2,)),
            dma((2, 3, 4)),
            dma((2, 3, 4, 2)),
            dma((2, 4)),
            dma((2, 4)),
            dma((2, 4)),
        ],
        compiler_params=pltpu.CompilerParams(
            collective_id=0, has_side_effects=True, vmem_limit_bytes=54400 << 10
        ),
        name="reduce_levels",
    )(kernel_shard, sketch, projections, inverses)
    return pl.pallas_call(
        last_kernel,
        out_shape=jax.ShapeDtypeStruct((2, 3, 128, 256), F32),
        in_specs=[vmem] * 7,
        out_specs=hbm,
        scratch_shapes=[pltpu.VMEM((3, 2, 128, 256), F32), dma((3,))],
        compiler_params=pltpu.CompilerParams(vmem_limit_bytes=8 << 20),
        name="last_level",
    )(*current, norm_gain.reshape(1, 256))


def solution(mesh):
    torus = Mesh(mesh.devices.reshape(2, 4, 4, 2, 2), AXES)
    in_specs = (
        P(None, ("yl", "z"), ("x", "yh", "c")),
        P(None, ("x", "yh", "c"), None),
        P(None, ("yl", "z"), None, None, None),
        P(None, ("yl", "z"), None, None, None),
        P(),
    )
    return jax.shard_map(
        shards, mesh=torus, in_specs=in_specs, out_specs=P(None, None, AXES, None), check_vma=False
    )
```

```python
import jax
import jax.numpy as jnp
from jax import lax
from jax.experimental import pallas as pl
from jax.experimental.pallas import tpu as pltpu
from jax.sharding import Mesh
from jax.sharding import PartitionSpec as P

AXES = ("yl", "z", "x", "yh", "c")
MESH = pl.DeviceIdType.MESH
F32 = jnp.float32
BF16 = jnp.bfloat16
EPSILON = 1e-06
PASSES = 3
LAST = PASSES - 1


def complex_block(real, imag):
    upper = jnp.concatenate([real, imag], axis=1)
    lower = jnp.concatenate([-imag, real], axis=1)
    return jnp.concatenate([upper, lower], axis=0)


def dot(a, b):
    return jnp.dot(a, b, preferred_element_type=F32)


def span(p, h):
    return pl.ds(h * 64, 64) if p == LAST else pl.ds(0, 128)


def reduce_kernel(
    k_hbm, s_hbm, proj_hbm, inv_hbm, *refs,
):
    outs = refs[:6]
    (
        kv, sv, pair, single, projv, invv, mats, mats_far, last_mats,
        own, c_send, c_recv, x_send, x_recv,
        mine, y1_send, y1_recv, held, y2_send, y2_recv, own1, z_recv, near_last,
        k_sem, s_sem, w_sem, m_sems, c_sems, x_sems, y1_sems, y2_sems, z_sems,
) = refs[6:]
    yl, z, x, yh, c = (lax.axis_index(a) for a in AXES)
    far_x = lax.rem(x + 2, 4)
    right = lax.rem(x + 1, 4)
    left = lax.rem(x + 3, 4)
    core_peer = (yl, z, x, yh, 1 - c)
    right_peer = (yl, z, right, yh, c)
    left_peer = (yl, z, left, yh, c)
    y1_peer = (1 - yl, z, x, 1 - yh, c)
    y2_peer = (1 - yl, z, x, yh, c)
    z_peer = (yl, lax.rem(z + 2, 4), x, yh, c)

    units = (
        ((far_x, 0), (far_x, 1)),
        ((right, 1), (left, 0)),
        ((right, 0), (left, 1)),
        ((x, 0), (x, 1)),
    )

    def start_slab(j):
        def start_half(half, _):
            core = 1 - c + half * (2 * c - 1)
            for part in range(2):
                for u in range(2):
                    dest_x, dest_yh = units[j][u]
                    row = pl.multiple_of(((dest_x * 2 + dest_yh) * 2 + core) * 128, 128)
                    near = pl.multiple_of((half * 2 + u) * 128, 128)
                    pltpu.make_async_copy(
                        k_hbm.at[part, pl.ds(row, 128), :],
                        kv.at[j, part, pl.ds(near, 128), :],
                        k_sem.at[j, half],
                    ).start()
            return 0

        lax.fori_loop(0, 2, start_half, 0)

    def wait_slab(j, half):
        pltpu.make_async_copy(
            k_hbm.at[:, pl.ds(0, 256), :],
            kv.at[j, :, pl.ds(half * 256, 256), :],
            k_sem.at[j, half],
        ).wait()

    def s_copy(p):
        return pltpu.make_async_copy(s_hbm.at[p], sv.at[p], s_sem.at[p])

    proj_copy = pltpu.make_async_copy(proj_hbm, projv, w_sem.at[0])
    inv_copy = pltpu.make_async_copy(inv_hbm, invv, w_sem.at[1])

    def remote(src, dst, sems, index, peer):
        return pltpu.make_async_remote_copy(
            src_ref=src,
            dst_ref=dst,
            send_sem=sems.at[(0,) + index],
            recv_sem=sems.at[(1,) + index],
            device_id=peer,
            device_id_type=MESH,
        )

    def m_copy():
        return remote(mats, mats_far, m_sems, (), y2_peer)

    def c_copy(p, j):
        return remote(c_send.at[p, j], c_recv.at[p, j], c_sems, (p, j), core_peer)

    def x_copy(p, j, u, h=0):
        peer = (right_peer, left_peer)[u]
        rows = span(p, h) if j == 2 else pl.ds(0, 128)
        at = (p, j, u, rows)
        return remote(x_send.at[at], x_recv.at[at], x_sems, (p, j + h, u), peer)

    def y1_copy(p, h):
        at = (p, span(p, h))
        return remote(y1_send.at[at], y1_recv.at[at], y1_sems, (p + h,), y1_peer)

    def y2_copy(p, h):
        at = (p, span(p, h))
        return remote(y2_send.at[at], y2_recv.at[at], y2_sems, (p + h,), y2_peer)

    def z_copy(p, h):
        at = (p, span(p, h))
        return remote(own1.at[at], z_recv.at[at], z_sems, (p + h,), z_peer)

    proj_copy.start()
    s_copy(0).start()
    s_copy(1).start()
    inv_copy.start()
    start_slab(0)
    start_slab(1)
    start_slab(2)
    start_slab(3)
    s_copy(2).start()

    barrier = pltpu.get_barrier_semaphore()
    for peer in (core_peer, right_peer, left_peer, y1_peer, y2_peer, z_peer):
        pl.semaphore_signal(barrier, inc=1, device_id=peer, device_id_type=MESH)

    proj_copy.wait()
    s_copy(0).wait()
    s_copy(1).wait()
    both = jnp.concatenate([projv[0, 0, 0], projv[0, 0, 1]], axis=1)
    for step in range(4):
        rows = pl.ds(step * 512, 512)
        first = dot(sv[0, rows, :], both).astype(BF16)
        second = dot(sv[1, rows, :], both).astype(BF16)
        real = jnp.concatenate([first[:, :128], second[:, :128]], axis=1)
        imag = jnp.concatenate([first[:, 128:], second[:, 128:]], axis=1)
        pair[0, rows, :] = real
        pair[1, rows, :] = imag
        pair[2, rows, :] = real + imag

    inv_copy.wait()
    level = complex_block(projv[1, 0, 0], projv[1, 0, 1])
    for i in range(2):
        rows = pl.ds(i * 128, 128)
        first = complex_block(invv[0, 0, 0, rows, :], invv[0, 0, 1, rows, :])
        mats[i] = dot(first, level).astype(BF16)
        last_mats[i] = complex_block(invv[1, 0, 0, rows, :], invv[1, 0, 1, rows, :])

    def project_last():
        s_copy(LAST).wait()
        both = jnp.concatenate([projv[0, 0, 0], projv[0, 0, 1]], axis=1)
        for step in range(4):
            rows = pl.ds(step * 512, 512)
            part = dot(sv[LAST, rows, :], both).astype(BF16)
            single[0, rows, :] = part
            single[1, rows, :] = jnp.concatenate([-part[:, 128:], part[:, :128]], axis=1)

    def post(p, j):
        copy = c_copy(p, j)
        copy.wait_send()
        copy.wait_recv()
        if j == 2:
            for u in range(2):
                x_copy(p, 0, u).wait_recv()
        for h in range(2 if p == LAST and j == 2 else 1):
            for u in range(2):
                rows = span(p, h) if j == 2 else pl.ds(0, 128)
                near = pl.ds(u * 128 + rows.start, rows.size)
                unit = own[p, j, near, :] + c_recv[p, j, near, :].astype(F32)
                if j == 2:
                    unit = unit + x_recv[p, 0, u, rows, :].astype(F32)
                x_send[p, j, u, rows, :] = unit.astype(BF16)
                x_copy(p, j, u, h).start()

    def finish_x(p, h):
        if h == 0:
            copy = c_copy(p, 3)
            copy.wait_send()
            copy.wait_recv()
            for u in range(2):
                x_copy(p, 1, u).wait_recv()
        for u in range(2):
            x_copy(p, 2, u, h).wait_recv()
        rows = span(p, h)

        def total(u):
            near = pl.ds(pl.multiple_of(u * 128 + rows.start, rows.size), rows.size)
            return (
                own[p, 3, near, :]
                + c_recv[p, 3, near, :].astype(F32)
                + x_recv[p, 2 - u, 0, rows, :].astype(F32)
                + x_recv[p, 1 + u, 1, rows, :].astype(F32)
            ).astype(BF16)

        y1_send[p, rows, :] = total(1 - yh)
        y1_copy(p, h).start()
        mine[p, rows, :] = total(yh)

    def level_products(p, h):
        y1_copy(p, h).wait_recv()
        rows = span(p, h)
        near = mine[p, rows, :]
        other = y1_recv[p, rows, :]
        y2_send[p, rows, :] = (dot(near, mats_far[1]) + dot(other, mats_far[0])).astype(BF16)
        y2_copy(p, h).start()
        held[p, rows, :] = dot(near, mats[0]) + dot(other, mats[1])

    def level_own(p, h):
        y2_copy(p, h).wait_recv()
        rows = span(p, h)
        value = (held[p, rows, :] + y2_recv[p, rows, :].astype(F32)).astype(BF16)
        own1[p, rows, :] = value
        z_copy(p, h).start()
        near_last[p, rows, :] = dot(value, last_mats[0])

    def finish(p, h):
        z_copy(p, h).wait_recv()
        rows = span(p, h)
        value = near_last[p, rows, :] + dot(z_recv[p, rows, :], last_mats[1])
        outs[2 * p][rows, :] = value[:, :256]
        outs[2 * p + 1][rows, :] = value[:, 256:]

    def pair_slab(j, _):
        wait_slab(j, 0)
        wait_slab(j, 1)
        real_part = dot(kv[j, 0], pair[0])
        imag_part = dot(kv[j, 1], pair[1])
        cross = dot(kv[j, 0] + kv[j, 1], pair[2])
        real = real_part - imag_part
        imag = cross - real_part - imag_part
        for p in range(2):
            cols = slice(p * 128, (p + 1) * 128)
            acc = jnp.concatenate([real[:, cols], imag[:, cols]], axis=1)
            c_send[p, j] = acc[:256].astype(BF16)
            own[p, j] = acc[256:]

        @pl.when(j == 0)
        def _():
            pl.semaphore_wait(barrier, 6)

        for p in range(2):
            c_copy(p, j).start()

        @pl.when(j == 0)
        def _():
            m_copy().start()
            post(0, 0)
            post(1, 0)

        for done in (1, 2):

            @pl.when(j == done + 1)
            def _():
                post(0, done)
                post(1, done)

        @pl.when(j == 2)
        def _():
            project_last()

        return 0

    def single_slab(j, _):
        acc = dot(kv[j, 0], single[0]) + dot(kv[j, 1], single[1])
        c_send[LAST, j] = acc[:256].astype(BF16)
        c_copy(LAST, j).start()
        own[LAST, j] = acc[256:]

        for done in range(3):

            @pl.when(j == done + 1)
            def _():
                post(LAST, done)

        for p in range(2):

            @pl.when(j == p + 1)
            def _():
                finish_x(p, 0)

        return 0

    lax.fori_loop(0, 4, pair_slab, 0)
    lax.fori_loop(0, 4, single_slab, 0)
    m_copy().wait()
    level_products(0, 0)
    finish_x(LAST, 0)
    level_products(1, 0)
    finish_x(LAST, 1)
    level_own(0, 0)
    level_products(LAST, 0)
    level_own(1, 0)
    level_products(LAST, 1)
    finish(0, 0)
    level_own(LAST, 0)
    level_own(LAST, 1)
    finish(1, 0)
    finish(LAST, 0)
    finish(LAST, 1)
    for p in range(PASSES):
        for u in range(2):
            for j in range(3):
                x_copy(p, j, u).wait_send()
        y1_copy(p, 0).wait_send()
        y2_copy(p, 0).wait_send()
        z_copy(p, 0).wait_send()
    for u in range(2):
        x_copy(LAST, 2, u, 1).wait_send()
    y1_copy(LAST, 1).wait_send()
    y2_copy(LAST, 1).wait_send()
    z_copy(LAST, 1).wait_send()


def last_kernel(*refs):
    gain, o_hbm, outv, o_sem = refs[6:]

    def o_copy(p):
        return pltpu.make_async_copy(outv.at[p], o_hbm.at[:, p], o_sem.at[p])

    for p in range(PASSES):
        real, imag = refs[2 * p][...], refs[2 * p + 1][...]
        power = jnp.sum(real * real + imag * imag, axis=-1, keepdims=True) / 256
        scale = lax.rsqrt(power + EPSILON)
        outv[p, 0] = real * scale * gain[...]
        outv[p, 1] = imag * scale * gain[...]
        o_copy(p).start()
    for p in range(PASSES):
        o_copy(p).wait()


def shards(kernel_shard, sketch, projections, inverses, norm_gain):
    dma = pltpu.SemaphoreType.DMA
    vmem = pl.BlockSpec(memory_space=pltpu.VMEM)
    hbm = pl.BlockSpec(memory_space=pl.ANY)
    current = pl.pallas_call(
        reduce_kernel,
        out_shape=[jax.ShapeDtypeStruct((128, 256), F32)] * 6,
        in_specs=[hbm] * 4,
        out_specs=[vmem] * 6,
        scratch_shapes=[
            pltpu.VMEM((4, 2, 512, 2048), BF16),
            pltpu.VMEM((3, 2048, 256), BF16),
            pltpu.VMEM((3, 2048, 256), BF16),
            pltpu.VMEM((2, 2048, 256), BF16),
            pltpu.VMEM((2, 1, 2, 256, 128), BF16),
            pltpu.VMEM((2, 1, 2, 256, 256), BF16),
            pltpu.VMEM((2, 256, 256), BF16),
            pltpu.VMEM((2, 256, 256), BF16),
            pltpu.VMEM((2, 256, 512), BF16),
            pltpu.VMEM((3, 4, 256, 256), F32),
            pltpu.VMEM((3, 4, 256, 256), BF16),
            pltpu.VMEM((3, 4, 256, 256), BF16),
            pltpu.VMEM((3, 3, 2, 128, 256), BF16),
            pltpu.VMEM((3, 3, 2, 128, 256), BF16),
            pltpu.VMEM((3, 128, 256), BF16),
            pltpu.VMEM((3, 128, 256), BF16),
            pltpu.VMEM((3, 128, 256), BF16),
            pltpu.VMEM((3, 128, 256), F32),
            pltpu.VMEM((3, 128, 256), BF16),
            pltpu.VMEM((3, 128, 256), BF16),
            pltpu.VMEM((3, 128, 256), BF16),
            pltpu.VMEM((3, 128, 256), BF16),
            pltpu.VMEM((3, 128, 512), F32),
            dma((4, 2)),
            dma((3,)),
            dma((2,)),
            dma((2,)),
            dma((2, 3, 4)),
            dma((2, 3, 4, 2)),
            dma((2, 4)),
            dma((2, 4)),
            dma((2, 4)),
        ],
        compiler_params=pltpu.CompilerParams(
            collective_id=0, has_side_effects=True, vmem_limit_bytes=54400 << 10
        ),
        name="reduce_levels",
    )(kernel_shard, sketch, projections, inverses)
    return pl.pallas_call(
        last_kernel,
        out_shape=jax.ShapeDtypeStruct((2, 3, 128, 256), F32),
        in_specs=[vmem] * 7,
        out_specs=hbm,
        scratch_shapes=[pltpu.VMEM((3, 2, 128, 256), F32), dma((3,))],
        compiler_params=pltpu.CompilerParams(vmem_limit_bytes=8 << 20),
        name="last_level",
    )(*current, norm_gain.reshape(1, 256))


def solution(mesh):
    torus = Mesh(mesh.devices.reshape(2, 4, 4, 2, 2), AXES)
    in_specs = (
        P(None, ("yl", "z"), ("x", "yh", "c")),
        P(None, ("x", "yh", "c"), None),
        P(None, ("yl", "z"), None, None, None),
        P(None, ("yl", "z"), None, None, None),
        P(),
    )
    return jax.shard_map(
        shards, mesh=torus, in_specs=in_specs, out_specs=P(None, None, AXES, None), check_vma=False
    )
```
